32 devices in a mesh: sweep: 2 (over x), recv: 16 (over z, y, core).
Axes of the slice: x: 2, y: 2, z: 4, core: 2. Of those that a mesh axis runs over, the one named last changes fastest.
Arguments:
- records: bfloat16 [16, 1024, 4096], P('sweep', 'recv'), may hold values from -6 to 6
- pilots: bfloat16 [16, 3968], replicated, may hold values from -0.09375 to 0.09375
- hadamard: int32 [16, 16], replicated, may hold values from -1 to 1, as said below
- code_vibrator: int32 [16], replicated, may hold values from 0 to 15, each once
- owner_map: int32 [1024], P('recv'), may hold values from 0 to 15
- live_mask: int32 [1024], P('recv'), may hold values 0 or 1
- filters: bfloat16 [16, 128, 128], P('sweep'), may hold values from -0.5 to 0.5
- targets: bfloat16 [16, 1024, 128], P('sweep', 'recv'), may hold values from -6 to 6
Outputs:
- responses: float32 [16, 1024, 128], P('sweep', 'recv')
- gradient: float32 [16, 128, 128], P('sweep', 'recv')
The draws below stay inside these ranges and needn't reach their ends.
Inputs may be any that keep to these rules, and one draw needn't show every extreme that they name: hadamard transposed times hadamard is 16 times the identity. `code_vibrator`: every vibrator belongs to exactly one code.
All inputs are finite; a program needn't handle non-finite values. No bound on the sum of `live_mask` on one device may be relied on, other than what follows from the above.
Results may differ from the reference program's by a relative error of at most 0.0085.
Values may be sent and summed in bfloat16 or wider, within the bound.
No kernel may reach another device: no remote copies, remote signals or barrier semaphores. Data moves between devices by JAX's collectives and lax.ppermute only.
A program may use at most 64 MiB of HBM per device.

```python
import math
import jax
import jax.numpy as jnp
from jax import lax

CODES = 16
NT = 4096
NLAG = 128
LP = 3968
RECEIVERS = 1024


def draw_hadamard(key, part):
    subkeys = jax.random.split(jax.random.fold_in(key, 71), 3)
    indices = jnp.arange(CODES, dtype=jnp.int32)
    common_bits = indices[:, None] & indices[None, :]
    parity = jnp.zeros((CODES, CODES), jnp.int32)
    for bit_pos in range(CODES.bit_length() - 1):
        parity = parity + (common_bits >> bit_pos & 1)
    sylvester = 1 - 2 * (parity % 2)
    row_signs = 2 * jax.random.randint(subkeys[0], (CODES,), 0, 2) - 1
    col_signs = 2 * jax.random.randint(subkeys[1], (CODES,), 0, 2) - 1
    row_order = jax.random.permutation(subkeys[2], CODES)
    signed = sylvester[row_order] * row_signs[:, None] * col_signs[None, :]
    return signed.astype(jnp.int32)


def place_ends(array, key, smallest, top_value):
    longest = array.shape.index(max(array.shape))
    spots = []
    for shift in (0, 1):
        where = [jax.random.randint(jax.random.fold_in(key, axis), (), 0, length) for axis, length in enumerate(array.shape)]
        where[longest] = (where[longest] + shift) % array.shape[longest]
        spots.append(tuple(where))
    return array.at[spots[0]].set(smallest).at[spots[1]].set(top_value)


def block_levels(key, extent, cuts, least, high):
    def one(position, blocks):
        draws = jax.random.uniform(jax.random.fold_in(jax.random.fold_in(key, 6), position), (blocks,), jnp.float32, least / len(cuts), high / len(cuts))
        return jnp.repeat(jnp.exp(draws), extent[position] // blocks).reshape((-1,) + (1,) * (len(extent) - position - 1))

    loudness = one(*cuts[0])
    for cut in cuts[1:]:
        loudness = loudness * one(*cut)
    return loudness


def scatter_about(rng, shape, spread, most, cuts=(), held_as=jnp.bfloat16):
    factor_of = block_levels(rng, shape, cuts, -0.22, 0.18) if cuts else 1.0
    drawn = jax.random.normal(rng, shape, jnp.float32) * spread * factor_of
    return jnp.minimum(jnp.maximum(drawn, -most), most).astype(held_as)


def setup_inputs(seed: int = 0) -> dict:
    splits = jax.random.split(jax.random.key(seed), 9)
    records = scatter_about(splits[0], (CODES, RECEIVERS, NT), 1.0, 6.0, ((0, 2), (1, 16)))
    pilots = scatter_about(splits[1], (CODES, LP), LP ** -0.5, 0.09375)
    hadamard = draw_hadamard(jax.random.fold_in(splits[8], 71), 0)
    code_vibrator = jax.random.permutation(splits[3], CODES).astype(jnp.int32)
    owner_map = place_ends(jax.random.randint(splits[4], (RECEIVERS,), 0, CODES), jax.random.fold_in(splits[4], 1), 0, CODES - 1).astype(jnp.int32)
    live_mask = place_ends((jax.random.randint(splits[5], (RECEIVERS,), 0, 8) < 7).astype(jnp.int32), jax.random.fold_in(splits[5], 1), 0, 1)
    filters = scatter_about(splits[6], (CODES, NLAG, NLAG), NLAG ** -0.5, 0.5, ((0, 2),))
    targets = scatter_about(splits[7], (CODES, RECEIVERS, NLAG), 1.0, 6.0, ((0, 2), (1, 16)))
    return dict(records=records, pilots=pilots, hadamard=hadamard, code_vibrator=code_vibrator, owner_map=owner_map, live_mask=live_mask, filters=filters, targets=targets)


def toeplitz(sweep_pilot):
    padding = jnp.zeros((NT + 1 - sweep_pilot.shape[0],), sweep_pilot.dtype)
    extended = jnp.concatenate([sweep_pilot, padding])
    return jnp.tile(extended, NLAG)[:NLAG * NT].reshape(NLAG, NT)

def reference(records, pilots, hadamard, code_vibrator, owner_map, live_mask, filters, targets):
    onehot = (code_vibrator[:, None] == jnp.arange(CODES, dtype=jnp.int32)[None, :]).astype(jnp.float32)
    code_pilot = jnp.dot(onehot, pilots.astype(jnp.float32), precision=lax.Precision.HIGHEST)
    sign_table = hadamard.astype(jnp.float32)
    code_norm = 1.0 / math.sqrt(CODES)

    def per_code(operands):
        sign_col, sweep_pilot = operands
        combined = jnp.zeros((RECEIVERS, NT), jnp.float32)
        for sweep_index in range(CODES):
            combined = combined + sign_col[sweep_index] * records[sweep_index].astype(jnp.float32)
        toe_rows = toeplitz(sweep_pilot)
        lagged = lax.dot_general(combined, toe_rows, (((1,), (1,)), ((), ())), precision=lax.Precision.HIGHEST, preferred_element_type=jnp.float32)
        return code_norm * lagged
    decoded = lax.map(per_code, (sign_table.T, code_pilot))
    decoded_b = decoded.astype(jnp.bfloat16)
    dec_wide = decoded_b.astype(jnp.float32)
    responses = jnp.einsum('crl,clm->crm', dec_wide, filters.astype(jnp.float32), precision=lax.Precision.HIGHEST)
    owned = (owner_map[None, :] == code_vibrator[:, None]).astype(jnp.float32)
    weight = live_mask.astype(jnp.float32)[None, :] * (0.25 + owned)
    residual = (weight[:, :, None] * (responses - targets.astype(jnp.float32))).astype(jnp.bfloat16)
    gradient = jnp.einsum('crl,crm->clm', dec_wide, residual.astype(jnp.float32), precision=lax.Precision.HIGHEST)
    gradient = gradient * (1.0 / math.sqrt(RECEIVERS))
    return (responses, gradient)
```

```python
import functools
import math

import jax
import jax.numpy as jnp
from jax import lax
from jax.experimental import pallas as pl
from jax.experimental.pallas import tpu as pltpu
from jax.sharding import PartitionSpec as P

BF16 = jnp.bfloat16
F32 = jnp.float32
SMEM = pl.BlockSpec(memory_space=pltpu.SMEM)
VMEM = pl.BlockSpec(memory_space=pltpu.VMEM)
ANY = pl.BlockSpec(memory_space=pl.ANY)
SKEW = 16


def iota(shape, axis):
    return lax.broadcasted_iota(jnp.int32, shape, axis)


def decode_kernel(vib, hadamard, pilots, records, out, held, sems, mix, pilot_rows, skewed, total, *, step, width):
    sweeps, channels, samples = records.shape
    owned, _, lags = out.shape
    block = mix.shape[1] // sweeps
    shift = block.bit_length() - 1
    length = pilots.shape[1]
    chunks = samples // width
    groups = lax.axis_size("sweep")
    mine = lax.axis_index("sweep")
    group = lax.rem(mine + step, groups)
    first_sweep = mine * sweeps
    first_code = group * owned

    def fetch(k):
        cols = pl.ds(pl.multiple_of(k * width, width), width)
        return pltpu.make_async_copy(records.at[:, :, cols], held.at[:, :, cols], sems.at[k])

    for k in range(chunks):
        fetch(k).start()
    signs = hadamard[...].astype(F32).astype(BF16)
    all_sweeps, codes = hadamard.shape
    rows, cols = mix.shape
    pick_code = (iota((rows, codes), 1) == first_code + (iota((rows, codes), 0) >> shift)).astype(F32).astype(BF16)
    pick_sweep = (iota((all_sweeps, cols), 0) == first_sweep + (iota((all_sweeps, cols), 1) >> shift)).astype(F32).astype(BF16)
    by_code = lax.dot_general(pick_code, signs, (((1,), (1,)), ((), ())), preferred_element_type=F32).astype(BF16)
    spread = jnp.dot(by_code, pick_sweep, preferred_element_type=F32)
    same = (iota((rows, cols), 0) & (block - 1)) == (iota((rows, cols), 1) & (block - 1))
    mix[...] = jnp.where(same, spread, 0.0).astype(BF16)
    pilot_rows[:, :length] = pilots[...].astype(F32)
    pilot_rows[:, length:] = jnp.zeros((pilots.shape[0], samples - length), F32)
    for c in range(owned):
        row = pilot_rows[pl.ds(vib[first_code + c], 1), :]
        wide = jnp.broadcast_to(row, (SKEW, samples))
        skewed[c, :, :lags] = jnp.zeros((SKEW, lags), BF16)
        skewed[c, :, lags:] = pltpu.roll(wide, 0, 1, stride=1, stride_axis=0).astype(BF16)
    total[...] = jnp.zeros_like(total)

    def chunk(k, carry):
        fetch(k).wait()
        start = pl.multiple_of(k * width, width)
        mixed = []
        for h in range(channels // block):
            traces = held[:, h * block : (h + 1) * block, pl.ds(start, width)].reshape(cols, width)
            mixed.append(jnp.dot(mix[...], traces, preferred_element_type=F32).astype(BF16))
        for c in range(owned):
            lines = jnp.concatenate([m[c * block : (c + 1) * block] for m in mixed], axis=0)
            window = skewed[c, :, pl.ds(start, width + lags)]
            shifts = [window[:, lags - j : lags - j + width] for j in range(0, lags, SKEW)]
            total[c] += lax.dot_general(
                lines, jnp.concatenate(shifts, axis=0), (((1,), (1,)), ((), ())), preferred_element_type=F32
            )
        return carry

    lax.fori_loop(0, chunks, chunk, 0)
    out[...] = total[...].astype(out.dtype)


def decode(vib, hadamard, pilots, records, owned, lags, step, dtype):
    sweeps, channels, samples = records.shape
    block = min(channels, 256 // sweeps)
    width = 1024
    return pl.pallas_call(
        functools.partial(decode_kernel, step=step, width=width),
        out_shape=jax.ShapeDtypeStruct((owned, channels, lags), dtype),
        in_specs=[SMEM, VMEM, VMEM, ANY],
        out_specs=VMEM,
        scratch_shapes=[
            pltpu.VMEM((sweeps, channels, samples), BF16),
            pltpu.SemaphoreType.DMA((samples // width,)),
            pltpu.VMEM((owned * block, sweeps * block), BF16),
            pltpu.VMEM((pilots.shape[0], samples), F32),
            pltpu.VMEM((owned, SKEW, lags + samples), BF16),
            pltpu.VMEM((owned, channels, lags), F32),
        ],
        cost_estimate=pl.CostEstimate(flops=8 * 10**9, bytes_accessed=records.size * 2, transcendentals=0),
        name=f"decode_{step}",
    )(vib, hadamard, pilots, records)


def tail_kernel(vib, owner, live, own, *refs, parts, radix, norm, factor):
    others, (filters, targets, responses, keep), sends, terms = refs[:parts], refs[parts : parts + 4], refs[parts + 4 : -1], refs[-1]
    owned, channels, lags = own.shape
    first_code = lax.axis_index("sweep") * owned
    digit = lax.rem(lax.axis_index("recv"), radix)
    eye = iota((channels, channels), 0) == iota((channels, channels), 1)

    def column(row):
        return jnp.sum(jnp.where(eye, jnp.broadcast_to(row.astype(F32), (channels, channels)), 0.0), axis=1, keepdims=True)

    owner_col = column(owner[...])
    live_col = column(live[...])
    shares, _, share_rows, _ = terms.shape
    for c in range(owned):
        partial = own[c]
        for other in others:
            partial = partial + other[c].astype(F32)
        decoded = (norm * partial).astype(BF16)
        response = jnp.dot(decoded, filters[c], preferred_element_type=F32)
        responses[c] = response
        match = (owner_col == vib[first_code + c].astype(F32)).astype(F32)
        weight = live_col * (0.25 + match)
        residual = (weight * (response - targets[c].astype(F32))).astype(BF16)
        grad = factor * lax.dot_general(decoded, residual, (((0,), (0,)), ((), ())), preferred_element_type=F32)
        for d in range(shares):
            terms[d, c] = grad[d * share_rows : (d + 1) * share_rows]
    for hi in range(shares // radix):
        keep[hi] = terms[hi * radix + digit]
        for k, send in enumerate(sends):
            send[hi] = terms[hi * radix + peer(digit, k + 1, radix)].astype(BF16)


def peer(digit, k, radix):
    if radix & (radix - 1) == 0:
        return digit ^ k
    return lax.rem(digit + k, radix) if not isinstance(digit, int) else (digit + k) % radix


def radices(size):
    parts = []
    for want in (2, 4):
        if size % want == 0 and size > 1:
            parts.append(want)
            size //= want
    while size > 1:
        f = next(q for q in (2, 3, 5, 7, size) if size % q == 0)
        parts.append(f)
        size //= f
    return parts or [1]


def exchange(values, stride, radix, size):
    got = []
    for k, value in enumerate(values):
        pairs = []
        for i in range(size):
            d = i // stride % radix
            pairs.append((i, i + (peer(d, k + 1, radix) - d) * stride))
        got.append(lax.ppermute(value, "recv", pairs))
    return got


def local(records, pilots, hadamard, code_vibrator, owner_map, live_mask, filters, targets):
    groups = lax.axis_size("sweep")
    size = lax.axis_size("recv")
    codes = hadamard.shape[1]
    owned, lags, _ = filters.shape
    channels = records.shape[1]
    received = []
    for step in range(1, groups):
        part = decode(code_vibrator, hadamard, pilots, records, owned, lags, step, BF16)
        received.append(lax.ppermute(part, "sweep", [(i, (i + step) % groups) for i in range(groups)]))
    own = decode(code_vibrator, hadamard, pilots, records, owned, lags, 0, F32)
    steps = radices(size)
    share_rows = lags // size
    piece = (size // steps[0], owned, share_rows, lags)
    outs = pl.pallas_call(
        functools.partial(
            tail_kernel,
            parts=len(received),
            radix=steps[0],
            norm=1.0 / math.sqrt(codes),
            factor=1.0 / math.sqrt(channels * size),
        ),
        out_shape=[jax.ShapeDtypeStruct((owned, channels, lags), F32), jax.ShapeDtypeStruct(piece, F32)]
        + [jax.ShapeDtypeStruct(piece, BF16)] * (steps[0] - 1),
        in_specs=[SMEM] + [VMEM] * (5 + len(received)),
        out_specs=[VMEM] * (1 + steps[0]),
        scratch_shapes=[pltpu.VMEM((size, owned, share_rows, lags), F32)],
        name="tail",
    )(code_vibrator, owner_map.reshape(1, channels), live_mask.reshape(1, channels), own, *received, filters, targets)
    responses, held, sends = outs[0], outs[1], outs[2:]
    me = lax.axis_index("recv")
    stride = 1
    for radix, after in zip(steps, steps[1:] + [None]):
        for got in exchange(sends, stride, radix, size):
            held = held + got.astype(F32)
        stride *= radix
        if after is None:
            break
        digit = me // stride % after
        grid = held.reshape((held.shape[0] // after, after) + held.shape[1:])
        sends = [lax.dynamic_index_in_dim(grid, peer(digit, k, after), 1, keepdims=False).astype(BF16) for k in range(1, after)]
        held = lax.dynamic_index_in_dim(grid, digit, 1, keepdims=False)
    return (responses, held[0])


def solution(mesh):
    in_specs = (
        P("sweep", "recv", None),
        P(),
        P(),
        P(),
        P("recv"),
        P("recv"),
        P("sweep", None, None),
        P("sweep", "recv", None),
    )
    out_specs = (P("sweep", "recv", None), P("sweep", "recv", None))
    return jax.shard_map(local, mesh=mesh, in_specs=in_specs, out_specs=out_specs, check_vma=False)
```

```python
import functools
import math

import jax
import jax.numpy as jnp
from jax import lax
from jax.experimental import pallas as pl
from jax.experimental.pallas import tpu as pltpu
from jax.sharding import PartitionSpec as P

BF16 = jnp.bfloat16
F32 = jnp.float32
SMEM = pl.BlockSpec(memory_space=pltpu.SMEM)
VMEM = pl.BlockSpec(memory_space=pltpu.VMEM)
HBM = pl.BlockSpec(memory_space=pltpu.HBM)
SKEW = 16
VMEM_LIMIT = 28 * 2**20


def iota(shape, axis):
    return lax.broadcasted_iota(jnp.int32, shape, axis)


def decode_kernel(
    vib, hadamard, pilots, records, out, held, sems, mix, backward, skewed, mixed, shifted, vib_s, signs_v, pilots_v, *, step
):
    sweeps, channels, samples = records.shape
    owned, _, lags = out.shape
    block = mix.shape[1] // sweeps
    shift = block.bit_length() - 1
    vibrators, length = pilots.shape
    chunks, early = sems.shape[0] - 3, shifted.shape[0]
    width = samples // chunks
    mine = lax.axis_index("sweep")
    first_sweep = mine * sweeps
    first_code = lax.rem(mine + step, lax.axis_size("sweep")) * owned

    def fetch(k):
        cols = pl.ds(k * width, width)
        return pltpu.make_async_copy(records.at[:, :, cols], held.at[:, :, cols], sems.at[k])

    small = [(hadamard, signs_v), (pilots, pilots_v), (vib, vib_s)]
    small = [pltpu.make_async_copy(x, y, sems.at[chunks + i]) for i, (x, y) in enumerate(small)]
    for copy in small:
        copy.start()
    for k in range(chunks):
        fetch(k).start()

    small[0].wait()
    signs = signs_v[...].astype(F32).astype(BF16)
    all_sweeps, codes = hadamard.shape
    rows, cols = mix.shape
    pick_code = (iota((rows, codes), 1) == first_code + (iota((rows, codes), 0) >> shift)).astype(F32).astype(BF16)
    pick_sweep = (iota((all_sweeps, cols), 0) == first_sweep + (iota((all_sweeps, cols), 1) >> shift)).astype(F32).astype(BF16)
    by_code = lax.dot_general(pick_code, signs, (((1,), (1,)), ((), ())), preferred_element_type=F32).astype(BF16)
    spread = jnp.dot(by_code, pick_sweep, preferred_element_type=F32)
    same = (iota((rows, cols), 0) & (block - 1)) == (iota((rows, cols), 1) & (block - 1))
    mix[...] = jnp.where(same, spread, 0.0).astype(BF16)

    small[1].wait()
    flip = (iota((lags, lags), 0) + iota((lags, lags), 1) == lags - 1).astype(F32).astype(BF16)
    pieces = jnp.concatenate([pilots_v[:, j : j + lags] for j in range(0, length, lags)], axis=0)
    pieces = jnp.dot(pieces, flip, preferred_element_type=F32)
    for j in range(samples // lags + 1):
        source = (samples // lags - 1 - j) * vibrators
        inside = 0 <= source < pieces.shape[0]
        backward[:, j * lags : (j + 1) * lags] = (
            pieces[source : source + vibrators] if inside else jnp.zeros((vibrators, lags), F32)
        )
    small[2].wait()
    made = 0

    def skew(upto):
        nonlocal made
        while made < min(upto, owned):
            row = backward[pl.ds(vib_s[first_code + made], 1), :]
            wide = jnp.broadcast_to(row, (SKEW, samples + lags))
            skewed[made] = pltpu.roll(wide, 1, 1, stride=1, stride_axis=0).astype(BF16)
            made += 1

    def shifts(c):
        phases = [skewed[c, :, lags - j : lags - j + samples] for j in range(0, lags, SKEW)]
        return jnp.concatenate(
            [p[:, samples - u - lags : samples - u] for u in range(0, samples, lags) for p in phases], axis=0
        )

    skew(2)
    for k in range(chunks):
        fetch(k).wait()
        for c in range(early * k // chunks, early * (k + 1) // chunks):
            skew(c + 1)
            shifted[c] = shifts(c)
        skew(2 + (owned - 2) * (k + 1) // chunks)
        for h in range(0, channels, block):
            traces = held[:, h : h + block, k * width : (k + 1) * width].reshape(cols, width)
            lines = jnp.dot(mix[...], traces, preferred_element_type=F32).astype(BF16)
            for c in range(owned):
                mixed[c, h : h + block, k * width : (k + 1) * width] = lines[c * block : (c + 1) * block]
    for c in range(owned):
        kernel = shifted[c] if c < early else shifts(c)
        out[c] = jnp.dot(mixed[c], kernel, preferred_element_type=F32).astype(out.dtype)


def decode(vib, hadamard, pilots, records, owned, lags, step, dtype):
    sweeps, channels, samples = records.shape
    block = min(channels, 256 // sweeps)
    chunks = 2
    early = min(4, owned)
    return pl.pallas_call(
        functools.partial(decode_kernel, step=step),
        out_shape=jax.ShapeDtypeStruct((owned, channels, lags), dtype),
        in_specs=[HBM] * 4,
        out_specs=VMEM,
        scratch_shapes=[
            pltpu.VMEM((sweeps, channels, samples), BF16),
            pltpu.SemaphoreType.DMA((chunks + 3,)),
            pltpu.VMEM((owned * block, sweeps * block), BF16),
            pltpu.VMEM((pilots.shape[0], samples + lags), F32),
            pltpu.VMEM((owned, SKEW, samples + lags), BF16),
            pltpu.VMEM((owned, channels, samples), BF16),
            pltpu.VMEM((early, samples, lags), BF16),
            pltpu.SMEM(vib.shape, jnp.int32),
            pltpu.VMEM(hadamard.shape, jnp.int32),
            pltpu.VMEM(pilots.shape, BF16),
        ],
        compiler_params=pltpu.CompilerParams(vmem_limit_bytes=VMEM_LIMIT),
        cost_estimate=pl.CostEstimate(flops=8 * 10**9, bytes_accessed=records.size * 2, transcendentals=0),
        name=f"decode_{step}",
    )(vib, hadamard, pilots, records)


def tail_kernel(vib, owner, live, own, *refs, parts, radix, norm, factor):
    others, (filters, targets, responses, keep), sends, terms = refs[:parts], refs[parts : parts + 4], refs[parts + 4 : -1], refs[-1]
    owned, channels, lags = own.shape
    first_code = lax.axis_index("sweep") * owned
    digit = lax.rem(lax.axis_index("recv"), radix)
    eye = iota((channels, channels), 0) == iota((channels, channels), 1)

    def column(row):
        return jnp.sum(jnp.where(eye, jnp.broadcast_to(row.astype(F32), (channels, channels)), 0.0), axis=1, keepdims=True)

    owner_col = column(owner[...])
    live_col = column(live[...])
    shares, _, share_rows, _ = terms.shape
    for c in range(owned):
        partial = own[c]
        for other in others:
            partial = partial + other[c].astype(F32)
        decoded = (norm * partial).astype(BF16)
        response = jnp.dot(decoded, filters[c], preferred_element_type=F32)
        responses[c] = response
        match = (owner_col == vib[first_code + c].astype(F32)).astype(F32)
        weight = live_col * (0.25 + match)
        residual = (weight * (response - targets[c].astype(F32))).astype(BF16)
        grad = factor * lax.dot_general(decoded, residual, (((0,), (0,)), ((), ())), preferred_element_type=F32)
        for d in range(shares):
            terms[d, c] = grad[d * share_rows : (d + 1) * share_rows]
    for hi in range(shares // radix):
        keep[hi] = terms[hi * radix + digit]
        for k, send in enumerate(sends):
            send[hi] = terms[hi * radix + peer(digit, k + 1, radix)].astype(BF16)


def peer(digit, k, radix):
    if radix & (radix - 1) == 0:
        return digit ^ k
    return lax.rem(digit + k, radix) if not isinstance(digit, int) else (digit + k) % radix


def radices(size):
    parts = []
    for want in (2, 4):
        if size % want == 0 and size > 1:
            parts.append(want)
            size //= want
    while size > 1:
        f = next(q for q in (2, 3, 5, 7, size) if size % q == 0)
        parts.append(f)
        size //= f
    return parts or [1]


def exchange(values, stride, radix, size):
    got = []
    for k, value in enumerate(values):
        pairs = []
        for i in range(size):
            d = i // stride % radix
            pairs.append((i, i + (peer(d, k + 1, radix) - d) * stride))
        got.append(lax.ppermute(value, "recv", pairs))
    return got


def local(records, pilots, hadamard, code_vibrator, owner_map, live_mask, filters, targets):
    groups = lax.axis_size("sweep")
    size = lax.axis_size("recv")
    codes = hadamard.shape[1]
    owned, lags, _ = filters.shape
    channels = records.shape[1]
    received = []
    for step in range(1, groups):
        part = decode(code_vibrator, hadamard, pilots, records, owned, lags, step, BF16)
        received.append(lax.ppermute(part, "sweep", [(i, (i + step) % groups) for i in range(groups)]))
    own = decode(code_vibrator, hadamard, pilots, records, owned, lags, 0, F32)
    steps = radices(size)
    share_rows = lags // size
    piece = (size // steps[0], owned, share_rows, lags)
    outs = pl.pallas_call(
        functools.partial(
            tail_kernel,
            parts=len(received),
            radix=steps[0],
            norm=1.0 / math.sqrt(codes),
            factor=1.0 / math.sqrt(channels * size),
        ),
        out_shape=[jax.ShapeDtypeStruct((owned, channels, lags), F32), jax.ShapeDtypeStruct(piece, F32)]
        + [jax.ShapeDtypeStruct(piece, BF16)] * (steps[0] - 1),
        in_specs=[SMEM] + [VMEM] * (5 + len(received)),
        out_specs=[VMEM] * (1 + steps[0]),
        scratch_shapes=[pltpu.VMEM((size, owned, share_rows, lags), F32)],
        compiler_params=pltpu.CompilerParams(vmem_limit_bytes=4 * 2**20),
        name="tail",
    )(code_vibrator, owner_map.reshape(1, channels), live_mask.reshape(1, channels), own, *received, filters, targets)
    responses, held, sends = outs[0], outs[1], outs[2:]
    me = lax.axis_index("recv")
    stride = 1
    for radix, after in zip(steps, steps[1:] + [None]):
        for got in exchange(sends, stride, radix, size):
            held = held + got.astype(F32)
        stride *= radix
        if after is None:
            break
        digit = me // stride % after
        grid = held.reshape((held.shape[0] // after, after) + held.shape[1:])
        sends = [lax.dynamic_index_in_dim(grid, peer(digit, k, after), 1, keepdims=False).astype(BF16) for k in range(1, after)]
        held = lax.dynamic_index_in_dim(grid, digit, 1, keepdims=False)
    return (responses, held[0])


def solution(mesh):
    in_specs = (
        P("sweep", "recv", None),
        P(),
        P(),
        P(),
        P("recv"),
        P("recv"),
        P("sweep", None, None),
        P("sweep", "recv", None),
    )
    out_specs = (P("sweep", "recv", None), P("sweep", "recv", None))
    return jax.shard_map(local, mesh=mesh, in_specs=in_specs, out_specs=out_specs, check_vma=False)
```

```python
import functools
import math

import jax
import jax.numpy as jnp
from jax import lax
from jax.experimental import pallas as pl
from jax.experimental.pallas import tpu as pltpu
from jax.sharding import PartitionSpec as P

BF16 = jnp.bfloat16
F32 = jnp.float32
SMEM = pl.BlockSpec(memory_space=pltpu.SMEM)
VMEM = pl.BlockSpec(memory_space=pltpu.VMEM)
HBM = pl.BlockSpec(memory_space=pltpu.HBM)
SKEW = 16
CHUNKS = 2
VMEM_LIMIT = 28 * 2**20


def iota(shape, axis):
    return lax.broadcasted_iota(jnp.int32, shape, axis)


def decode_kernel(*refs, step, first):
    if first:
        vib, hadamard, pilots, records, out, held, signs_v, ordered, mix, skewed, mixed, shifted, sems, vib_s, pilots_v, backward = refs
    else:
        held, signs_v, ordered, out, mix, skewed, mixed, shifted = refs
    sweeps, channels, samples = held.shape
    owned, _, lags = out.shape
    all_sweeps, codes = signs_v.shape
    block = mix.shape[1] // sweeps
    shift = block.bit_length() - 1
    early = shifted.shape[0]
    width = samples // CHUNKS
    mine = lax.axis_index("sweep")
    first_sweep = mine * sweeps
    first_code = lax.rem(mine + step, lax.axis_size("sweep")) * owned

    def fetch(k):
        cols = pl.ds(k * width, width)
        return pltpu.make_async_copy(records.at[:, :, cols], held.at[:, :, cols], sems.at[k])

    if first:
        small = [(hadamard, signs_v), (pilots, pilots_v), (vib, vib_s)]
        small = [pltpu.make_async_copy(x, y, sems.at[CHUNKS + i]) for i, (x, y) in enumerate(small)]
        for copy in small:
            copy.start()
        for k in range(CHUNKS):
            fetch(k).start()
        small[0].wait()

    signs = signs_v[...].astype(F32).astype(BF16)
    rows, cols = mix.shape
    pick_code = (iota((rows, codes), 1) == first_code + (iota((rows, codes), 0) >> shift)).astype(F32).astype(BF16)
    pick_sweep = (iota((all_sweeps, cols), 0) == first_sweep + (iota((all_sweeps, cols), 1) >> shift)).astype(F32).astype(BF16)
    by_code = lax.dot_general(pick_code, signs, (((1,), (1,)), ((), ())), preferred_element_type=F32).astype(BF16)
    spread = jnp.dot(by_code, pick_sweep, preferred_element_type=F32)
    same = (iota((rows, cols), 0) & (block - 1)) == (iota((rows, cols), 1) & (block - 1))
    mix[...] = jnp.where(same, spread, 0.0).astype(BF16)

    if first:
        small[1].wait()
        vibrators, length = pilots.shape
        flip = (iota((lags, lags), 0) + iota((lags, lags), 1) == lags - 1).astype(F32).astype(BF16)
        pieces = jnp.concatenate([pilots_v[:, j : j + lags] for j in range(0, length, lags)], axis=0)
        pieces = jnp.dot(pieces, flip, preferred_element_type=F32)
        for j in range(samples // lags + 1):
            source = (samples // lags - 1 - j) * vibrators
            inside = 0 <= source < pieces.shape[0]
            backward[:, j * lags : (j + 1) * lags] = (
                pieces[source : source + vibrators] if inside else jnp.zeros((vibrators, lags), F32)
            )
        small[2].wait()
        for c in range(codes):
            ordered[pl.ds(c, 1), :] = backward[pl.ds(vib_s[c], 1), :]
    made = 0

    def skew(upto):
        nonlocal made
        while made < min(upto, owned):
            row = ordered[pl.ds(first_code + made, 1), :]
            wide = jnp.broadcast_to(row, (SKEW, samples + lags))
            skewed[made] = pltpu.roll(wide, 1, 1, stride=1, stride_axis=0).astype(BF16)
            made += 1

    def shifts(c):
        phases = [skewed[c, :, lags - j : lags - j + samples] for j in range(0, lags, SKEW)]
        return jnp.concatenate(
            [p[:, samples - u - lags : samples - u] for u in range(0, samples, lags) for p in phases], axis=0
        )

    skew(2)
    for k in range(CHUNKS):
        if first:
            fetch(k).wait()
        for c in range(early * k // CHUNKS, early * (k + 1) // CHUNKS):
            skew(c + 1)
            shifted[c] = shifts(c)
        skew(2 + (owned - 2) * (k + 1) // CHUNKS)
        for h in range(0, channels, block):
            traces = held[:, h : h + block, k * width : (k + 1) * width].reshape(cols, width)
            lines = jnp.dot(mix[...], traces, preferred_element_type=F32).astype(BF16)
            for c in range(owned):
                mixed[c, h : h + block, k * width : (k + 1) * width] = lines[c * block : (c + 1) * block]
    for c in range(owned):
        kernel = shifted[c] if c < early else shifts(c)
        out[c] = jnp.dot(mixed[c], kernel, preferred_element_type=F32).astype(out.dtype)


def decode(inputs, shape, owned, codes, lags, step, dtype, first):
    sweeps, channels, samples = shape
    block = min(channels, 256 // sweeps)
    early = min(4, owned)
    out_shape = [pltpu.VMEM((owned, channels, lags), dtype)]
    scratch = [
        pltpu.VMEM((owned * block, sweeps * block), BF16),
        pltpu.VMEM((owned, SKEW, samples + lags), BF16),
        pltpu.VMEM((owned, channels, samples), BF16),
        pltpu.VMEM((early, samples, lags), BF16),
    ]
    if first:
        vib, hadamard, pilots, _ = inputs
        inputs = [pltpu.with_memory_space_constraint(x, pltpu.HBM) for x in inputs]
        out_shape += [
            pltpu.VMEM(shape, BF16),
            pltpu.VMEM(hadamard.shape, jnp.int32),
            pltpu.VMEM((codes, samples + lags), F32),
        ]
        scratch += [
            pltpu.SemaphoreType.DMA((CHUNKS + 3,)),
            pltpu.SMEM(vib.shape, jnp.int32),
            pltpu.VMEM(pilots.shape, BF16),
            pltpu.VMEM((pilots.shape[0], samples + lags), F32),
        ]
    return pl.pallas_call(
        functools.partial(decode_kernel, step=step, first=first),
        out_shape=out_shape,
        in_specs=[HBM if first else VMEM] * len(inputs),
        out_specs=[VMEM] * len(out_shape),
        scratch_shapes=scratch,
        compiler_params=pltpu.CompilerParams(vmem_limit_bytes=VMEM_LIMIT),
        cost_estimate=pl.CostEstimate(flops=8 * 10**9, bytes_accessed=math.prod(shape) * 2, transcendentals=0),
        name=f"decode_{step}",
    )(*inputs)


def tail_kernel(vib, owner, live, own, *refs, parts, radix, norm, factor):
    others, (filters, targets, responses, keep), sends, terms = refs[:parts], refs[parts : parts + 4], refs[parts + 4 : -1], refs[-1]
    owned, channels, lags = own.shape
    first_code = lax.axis_index("sweep") * owned
    digit = lax.rem(lax.axis_index("recv"), radix)
    eye = iota((channels, channels), 0) == iota((channels, channels), 1)

    def column(row):
        return jnp.sum(jnp.where(eye, jnp.broadcast_to(row.astype(F32), (channels, channels)), 0.0), axis=1, keepdims=True)

    owner_col = column(owner[...])
    live_col = column(live[...])
    shares, _, share_rows, _ = terms.shape
    for c in range(owned):
        partial = own[c]
        for other in others:
            partial = partial + other[c].astype(F32)
        decoded = (norm * partial).astype(BF16)
        response = jnp.dot(decoded, filters[c], preferred_element_type=F32)
        responses[c] = response
        match = (owner_col == vib[first_code + c].astype(F32)).astype(F32)
        weight = live_col * (0.25 + match)
        residual = (weight * (response - targets[c].astype(F32))).astype(BF16)
        grad = factor * lax.dot_general(decoded, residual, (((0,), (0,)), ((), ())), preferred_element_type=F32)
        for d in range(shares):
            terms[d, c] = grad[d * share_rows : (d + 1) * share_rows]
    for hi in range(shares // radix):
        keep[hi] = terms[hi * radix + digit]
        for k, send in enumerate(sends):
            send[hi] = terms[hi * radix + peer(digit, k + 1, radix)].astype(BF16)


def peer(digit, k, radix):
    if radix & (radix - 1) == 0:
        return digit ^ k
    return lax.rem(digit + k, radix) if not isinstance(digit, int) else (digit + k) % radix


def radices(size):
    parts = []
    for want in (2, 4):
        if size % want == 0 and size > 1:
            parts.append(want)
            size //= want
    while size > 1:
        f = next(q for q in (2, 3, 5, 7, size) if size % q == 0)
        parts.append(f)
        size //= f
    return parts or [1]


def exchange(values, stride, radix, size):
    got = []
    for k, value in enumerate(values):
        pairs = []
        for i in range(size):
            d = i // stride % radix
            pairs.append((i, i + (peer(d, k + 1, radix) - d) * stride))
        got.append(lax.ppermute(value, "recv", pairs))
    return got


def local(records, pilots, hadamard, code_vibrator, owner_map, live_mask, filters, targets):
    groups = lax.axis_size("sweep")
    size = lax.axis_size("recv")
    codes = hadamard.shape[1]
    owned, lags, _ = filters.shape
    channels = records.shape[1]
    received = []
    inputs = (code_vibrator, hadamard, pilots, records)
    for step in list(range(1, groups)) + [0]:
        dtype = BF16 if step else F32
        part, *extra = decode(inputs, records.shape, owned, codes, lags, step, dtype, len(inputs) == 4)
        if extra:
            inputs = tuple(extra)
        if step:
            received.append(lax.ppermute(part, "sweep", [(i, (i + step) % groups) for i in range(groups)]))
    own = part
    steps = radices(size)
    share_rows = lags // size
    piece = (size // steps[0], owned, share_rows, lags)
    outs = pl.pallas_call(
        functools.partial(
            tail_kernel,
            parts=len(received),
            radix=steps[0],
            norm=1.0 / math.sqrt(codes),
            factor=1.0 / math.sqrt(channels * size),
        ),
        out_shape=[jax.ShapeDtypeStruct((owned, channels, lags), F32), jax.ShapeDtypeStruct(piece, F32)]
        + [jax.ShapeDtypeStruct(piece, BF16)] * (steps[0] - 1),
        in_specs=[SMEM] + [VMEM] * (5 + len(received)),
        out_specs=[VMEM] * (1 + steps[0]),
        scratch_shapes=[pltpu.VMEM((size, owned, share_rows, lags), F32)],
        compiler_params=pltpu.CompilerParams(vmem_limit_bytes=4 * 2**20),
        name="tail",
    )(code_vibrator, owner_map.reshape(1, channels), live_mask.reshape(1, channels), own, *received, filters, targets)
    responses, held, sends = outs[0], outs[1], outs[2:]
    me = lax.axis_index("recv")
    stride = 1
    for radix, after in zip(steps, steps[1:] + [None]):
        for got in exchange(sends, stride, radix, size):
            held = held + got.astype(F32)
        stride *= radix
        if after is None:
            break
        digit = me // stride % after
        grid = held.reshape((held.shape[0] // after, after) + held.shape[1:])
        sends = [lax.dynamic_index_in_dim(grid, peer(digit, k, after), 1, keepdims=False).astype(BF16) for k in range(1, after)]
        held = lax.dynamic_index_in_dim(grid, digit, 1, keepdims=False)
    return (responses, held[0])


def solution(mesh):
    in_specs = (
        P("sweep", "recv", None),
        P(),
        P(),
        P(),
        P("recv"),
        P("recv"),
        P("sweep", None, None),
        P("sweep", "recv", None),
    )
    out_specs = (P("sweep", "recv", None), P("sweep", "recv", None))
    return jax.shard_map(local, mesh=mesh, in_specs=in_specs, out_specs=out_specs, check_vma=False)
```

```python
import functools
import math

import jax
import jax.numpy as jnp
from jax import lax
from jax.experimental import pallas as pl
from jax.experimental.pallas import tpu as pltpu
from jax.sharding import PartitionSpec as P

BF16 = jnp.bfloat16
F32 = jnp.float32
SMEM = pl.BlockSpec(memory_space=pltpu.SMEM)
VMEM = pl.BlockSpec(memory_space=pltpu.VMEM)
HBM = pl.BlockSpec(memory_space=pltpu.HBM)
SKEW = 16
CHUNKS = 2
VMEM_LIMIT = 28 * 2**20


def iota(shape, axis):
    return lax.broadcasted_iota(jnp.int32, shape, axis)


def column(row):
    size = row.shape[1]
    eye = iota((size, size), 0) == iota((size, size), 1)
    return jnp.sum(jnp.where(eye, jnp.broadcast_to(row.astype(F32), (size, size)), 0.0), axis=1, keepdims=True)


def decode_kernel(*refs, step, first):
    if first:
        (vib, hadamard, pilots, owner, live, records), (out, held, signs_v, ordered, weight) = refs[:6], refs[6:11]
        mix, skewed, mixed, shifted, sems, vib_s, pilots_v, owner_v, live_v, backward = refs[11:]
    else:
        held, signs_v, ordered, out, mix, skewed, mixed, shifted = refs
    sweeps, channels, samples = held.shape
    owned, _, lags = out.shape
    all_sweeps, codes = signs_v.shape
    block = mix.shape[1] // sweeps
    shift = block.bit_length() - 1
    early = shifted.shape[0]
    width = samples // CHUNKS
    mine = lax.axis_index("sweep")
    first_sweep = mine * sweeps
    first_code = lax.rem(mine + step, lax.axis_size("sweep")) * owned

    def fetch(k):
        cols = pl.ds(k * width, width)
        return pltpu.make_async_copy(records.at[:, :, cols], held.at[:, :, cols], sems.at[k])

    if first:
        small = [(hadamard, signs_v), (pilots, pilots_v), (vib, vib_s), (owner, owner_v), (live, live_v)]
        small = [pltpu.make_async_copy(x, y, sems.at[CHUNKS + i]) for i, (x, y) in enumerate(small)]
        for copy in small:
            copy.start()
        for k in range(CHUNKS):
            fetch(k).start()
        small[0].wait()

    signs = signs_v[...].astype(F32).astype(BF16)
    rows, cols = mix.shape
    pick_code = (iota((rows, codes), 1) == first_code + (iota((rows, codes), 0) >> shift)).astype(F32).astype(BF16)
    pick_sweep = (iota((all_sweeps, cols), 0) == first_sweep + (iota((all_sweeps, cols), 1) >> shift)).astype(F32).astype(BF16)
    by_code = lax.dot_general(pick_code, signs, (((1,), (1,)), ((), ())), preferred_element_type=F32).astype(BF16)
    spread = jnp.dot(by_code, pick_sweep, preferred_element_type=F32)
    same = (iota((rows, cols), 0) & (block - 1)) == (iota((rows, cols), 1) & (block - 1))
    mix[...] = jnp.where(same, spread, 0.0).astype(BF16)

    if first:
        small[1].wait()
        vibrators, length = pilots.shape
        flip = (iota((lags, lags), 0) + iota((lags, lags), 1) == lags - 1).astype(F32).astype(BF16)
        pieces = jnp.concatenate([pilots_v[:, j : j + lags] for j in range(0, length, lags)], axis=0)
        pieces = jnp.dot(pieces, flip, preferred_element_type=F32)
        for j in range(samples // lags + 1):
            source = (samples // lags - 1 - j) * vibrators
            inside = 0 <= source < pieces.shape[0]
            backward[:, j * lags : (j + 1) * lags] = (
                pieces[source : source + vibrators] if inside else jnp.zeros((vibrators, lags), F32)
            )
        small[2].wait()
        for c in range(codes):
            ordered[pl.ds(c, 1), :] = backward[pl.ds(vib_s[c], 1), :]
        small[3].wait()
        small[4].wait()
        owner_c, live_c = column(owner_v[...]), column(live_v[...])
        for c in range(owned):
            match = (owner_c == vib_s[mine * owned + c].astype(F32)).astype(F32)
            weight[c] = jnp.broadcast_to(live_c * (0.25 + match), weight.shape[1:])
    made = 0

    def skew(upto):
        nonlocal made
        while made < min(upto, owned):
            row = ordered[pl.ds(first_code + made, 1), :]
            wide = jnp.broadcast_to(row, (SKEW, samples + lags))
            skewed[made] = pltpu.roll(wide, 1, 1, stride=1, stride_axis=0).astype(BF16)
            made += 1

    def shifts(c):
        phases = [skewed[c, :, lags - j : lags - j + samples] for j in range(0, lags, SKEW)]
        return jnp.concatenate(
            [p[:, samples - u - lags : samples - u] for u in range(0, samples, lags) for p in phases], axis=0
        )

    skew(2)
    for k in range(CHUNKS):
        if first:
            fetch(k).wait()
        for c in range(early * k // CHUNKS, early * (k + 1) // CHUNKS):
            skew(c + 1)
            shifted[c] = shifts(c)
        skew(2 + (owned - 2) * (k + 1) // CHUNKS)
        for h in range(0, channels, block):
            traces = held[:, h : h + block, k * width : (k + 1) * width].reshape(cols, width)
            lines = jnp.dot(mix[...], traces, preferred_element_type=F32).astype(BF16)
            for c in range(owned):
                mixed[c, h : h + block, k * width : (k + 1) * width] = lines[c * block : (c + 1) * block]
    for c in range(owned):
        kernel = shifted[c] if c < early else shifts(c)
        out[c] = jnp.dot(mixed[c], kernel, preferred_element_type=F32).astype(out.dtype)


def decode(inputs, shape, owned, codes, lags, step, dtype, first):
    sweeps, channels, samples = shape
    block = min(channels, 256 // sweeps)
    early = min(4, owned)
    out_shape = [pltpu.VMEM((owned, channels, lags), dtype)]
    scratch = [
        pltpu.VMEM((owned * block, sweeps * block), BF16),
        pltpu.VMEM((owned, SKEW, samples + lags), BF16),
        pltpu.VMEM((owned, channels, samples), BF16),
        pltpu.VMEM((early, samples, lags), BF16),
    ]
    if first:
        vib, hadamard, pilots, owner, live, _ = inputs
        inputs = [pltpu.with_memory_space_constraint(x, pltpu.HBM) for x in inputs]
        out_shape += [
            pltpu.VMEM(shape, BF16),
            pltpu.VMEM(hadamard.shape, jnp.int32),
            pltpu.VMEM((codes, samples + lags), F32),
            pltpu.VMEM((owned, channels, lags), F32),
        ]
        scratch += [
            pltpu.SemaphoreType.DMA((CHUNKS + 5,)),
            pltpu.SMEM(vib.shape, jnp.int32),
            pltpu.VMEM(pilots.shape, BF16),
            pltpu.VMEM(owner.shape, jnp.int32),
            pltpu.VMEM(live.shape, jnp.int32),
            pltpu.VMEM((pilots.shape[0], samples + lags), F32),
        ]
    return pl.pallas_call(
        functools.partial(decode_kernel, step=step, first=first),
        out_shape=out_shape,
        in_specs=[HBM if first else VMEM] * len(inputs),
        out_specs=[VMEM] * len(out_shape),
        scratch_shapes=scratch,
        compiler_params=pltpu.CompilerParams(vmem_limit_bytes=VMEM_LIMIT),
        cost_estimate=pl.CostEstimate(flops=8 * 10**9, bytes_accessed=math.prod(shape) * 2, transcendentals=0),
        name=f"decode_{step}",
    )(*inputs)


def orders(size):
    bits = list(range(1, size.bit_length() - 1))
    swapped = list(bits)
    for i in range(0, len(bits) - 1, 2):
        swapped[i], swapped[i + 1] = bits[i + 1], bits[i]
    return [0] + bits, [0] + swapped


def tail_kernel(weight, own, *refs, parts, norm, factor):
    others, (filters, targets, responses, keep, send, terms) = refs[:parts], refs[parts:]
    owned, channels, lags = own.shape
    shares, _, share_rows, _ = terms.shape
    for c in range(owned):
        partial = own[c]
        for other in others:
            partial = partial + other[c].astype(F32)
        decoded = (norm * partial).astype(BF16)
        response = jnp.dot(decoded, filters[c], preferred_element_type=F32)
        responses[c] = response
        residual = (weight[c] * (response - targets[c].astype(F32))).astype(BF16)
        grad = factor * lax.dot_general(decoded, residual, (((0,), (0,)), ((), ())), preferred_element_type=F32)
        for d in range(shares):
            terms[d, c] = grad[d * share_rows : (d + 1) * share_rows]
    parity = lax.rem(lax.axis_index("recv"), 2)
    even, odd = orders(shares)
    for i in range(shares // 2):
        places = [
            sum(1 << bit for j, bit in enumerate(reversed(order[1:])) if i >> j & 1) for order in (even, odd)
        ]
        mine, other = (places[0] + (places[1] - places[0]) * p for p in (parity, 1 - parity))
        keep[i] = terms[mine + parity]
        send[i] = terms[other + 1 - parity].astype(BF16)


def local(records, pilots, hadamard, code_vibrator, owner_map, live_mask, filters, targets):
    groups = lax.axis_size("sweep")
    size = lax.axis_size("recv")
    codes = hadamard.shape[1]
    owned, lags, _ = filters.shape
    channels = records.shape[1]
    received = []
    inputs = (code_vibrator, hadamard, pilots, owner_map.reshape(1, channels), live_mask.reshape(1, channels), records)
    first = True
    for step in list(range(1, groups)) + [0]:
        dtype = BF16 if step else F32
        part, *extra = decode(inputs, records.shape, owned, codes, lags, step, dtype, first)
        if first:
            *inputs, weight = extra
            first = False
        if step:
            received.append(lax.ppermute(part, "sweep", [(i, (i + step) % groups) for i in range(groups)]))
    share_rows = lags // size
    piece = (size // 2, owned, share_rows, lags)
    responses, held, sent = pl.pallas_call(
        functools.partial(
            tail_kernel, parts=len(received), norm=1.0 / math.sqrt(codes), factor=1.0 / math.sqrt(channels * size)
        ),
        out_shape=[pltpu.VMEM((owned, channels, lags), F32), pltpu.VMEM(piece, F32), pltpu.VMEM(piece, BF16)],
        in_specs=[VMEM] * (4 + len(received)),
        out_specs=[VMEM] * 3,
        scratch_shapes=[pltpu.VMEM((size, owned, share_rows, lags), F32)],
        compiler_params=pltpu.CompilerParams(vmem_limit_bytes=8 * 2**20),
        name="tail",
    )(weight, part, *received, filters, targets)
    me = lax.axis_index("recv")
    even, odd = orders(size)
    for j in range(len(even)):
        pairs = [(i, i ^ (1 << (odd if i & 1 else even)[j])) for i in range(size)]
        held = held + lax.ppermute(sent, "recv", pairs).astype(F32)
        if j + 1 < len(even):
            bit = jnp.where(me & 1 == 1, me >> odd[j + 1], me >> even[j + 1]) & 1
            half = held.shape[0] // 2
            sent = lax.dynamic_slice_in_dim(held, (1 - bit) * half, half, 0).astype(BF16)
            held = lax.dynamic_slice_in_dim(held, bit * half, half, 0)
    return (responses, held[0])


def solution(mesh):
    in_specs = (
        P("sweep", "recv", None),
        P(),
        P(),
        P(),
        P("recv"),
        P("recv"),
        P("sweep", None, None),
        P("sweep", "recv", None),
    )
    out_specs = (P("sweep", "recv", None), P("sweep", "recv", None))
    return jax.shard_map(local, mesh=mesh, in_specs=in_specs, out_specs=out_specs, check_vma=False)
```

```python
import functools
import math

import jax
import jax.numpy as jnp
from jax import lax
from jax.experimental import pallas as pl
from jax.experimental.pallas import tpu as pltpu
from jax.sharding import PartitionSpec as P

BF16 = jnp.bfloat16
F32 = jnp.float32
SMEM = pl.BlockSpec(memory_space=pltpu.SMEM)
VMEM = pl.BlockSpec(memory_space=pltpu.VMEM)
HBM = pl.BlockSpec(memory_space=pltpu.HBM)
SKEW = 16
CHUNKS = 2
VMEM_LIMIT = 28 * 2**20


def iota(shape, axis):
    return lax.broadcasted_iota(jnp.int32, shape, axis)


def column(row):
    size = row.shape[1]
    eye = iota((size, size), 0) == iota((size, size), 1)
    return jnp.sum(jnp.where(eye, jnp.broadcast_to(row.astype(F32), (size, size)), 0.0), axis=1, keepdims=True)


def decode_kernel(*refs, step, first):
    if first:
        (vib, hadamard, pilots, owner, live, records), (out, held, signs_v, ordered, weight) = refs[:6], refs[6:11]
        mix, skewed, mixed, shifted, sems, vib_s, pilots_v, owner_v, live_v, backward = refs[11:]
    else:
        held, signs_v, ordered, out, mix, skewed, mixed, shifted = refs
    sweeps, channels, samples = held.shape
    owned, _, lags = out.shape
    all_sweeps, codes = signs_v.shape
    block = mix.shape[1] // sweeps
    shift = block.bit_length() - 1
    early = shifted.shape[0]
    width = samples // CHUNKS
    mine = lax.axis_index("sweep")
    first_sweep = mine * sweeps
    first_code = lax.rem(mine + step, lax.axis_size("sweep")) * owned

    def fetch(k):
        cols = pl.ds(k * width, width)
        return pltpu.make_async_copy(records.at[:, :, cols], held.at[:, :, cols], sems.at[k])

    if first:
        small = [(hadamard, signs_v), (pilots, pilots_v), (vib, vib_s), (owner, owner_v), (live, live_v)]
        small = [pltpu.make_async_copy(x, y, sems.at[CHUNKS + i]) for i, (x, y) in enumerate(small)]
        for copy in small:
            copy.start()
        for k in range(CHUNKS):
            fetch(k).start()
        small[0].wait()

    signs = signs_v[...].astype(F32).astype(BF16)
    rows, cols = mix.shape
    pick_code = (iota((rows, codes), 1) == first_code + (iota((rows, codes), 0) >> shift)).astype(F32).astype(BF16)
    pick_sweep = (iota((all_sweeps, cols), 0) == first_sweep + (iota((all_sweeps, cols), 1) >> shift)).astype(F32).astype(BF16)
    by_code = lax.dot_general(pick_code, signs, (((1,), (1,)), ((), ())), preferred_element_type=F32).astype(BF16)
    spread = jnp.dot(by_code, pick_sweep, preferred_element_type=F32)
    same = (iota((rows, cols), 0) & (block - 1)) == (iota((rows, cols), 1) & (block - 1))
    mix[...] = jnp.where(same, spread, 0.0).astype(BF16)

    if first:
        small[1].wait()
        vibrators, length = pilots.shape
        flip = (iota((lags, lags), 0) + iota((lags, lags), 1) == lags - 1).astype(F32).astype(BF16)
        pieces = jnp.concatenate([pilots_v[:, j : j + lags] for j in range(0, length, lags)], axis=0)
        pieces = jnp.dot(pieces, flip, preferred_element_type=F32)
        for j in range(samples // lags + 1):
            source = (samples // lags - 1 - j) * vibrators
            inside = 0 <= source < pieces.shape[0]
            backward[:, j * lags : (j + 1) * lags] = (
                pieces[source : source + vibrators] if inside else jnp.zeros((vibrators, lags), F32)
            )
        small[2].wait()
        for c in range(codes):
            ordered[pl.ds(c, 1), :] = backward[pl.ds(vib_s[c], 1), :]
        small[3].wait()
        small[4].wait()
        owner_c, live_c = column(owner_v[...]), column(live_v[...])
        for c in range(owned):
            match = (owner_c == vib_s[mine * owned + c].astype(F32)).astype(F32)
            weight[c] = jnp.broadcast_to(live_c * (0.25 + match), weight.shape[1:])
    made = 0

    def skew(upto):
        nonlocal made
        while made < min(upto, owned):
            row = ordered[pl.ds(first_code + made, 1), :]
            wide = jnp.broadcast_to(row, (SKEW, samples + lags))
            skewed[made] = pltpu.roll(wide, 1, 1, stride=1, stride_axis=0).astype(BF16)
            made += 1

    def shifts(c):
        phases = [skewed[c, :, lags - j : lags - j + samples] for j in range(0, lags, SKEW)]
        return jnp.concatenate(
            [p[:, samples - u - lags : samples - u] for u in range(0, samples, lags) for p in phases], axis=0
        )

    skew(2)
    for k in range(CHUNKS):
        if first:
            fetch(k).wait()
        for c in range(early * k // CHUNKS, early * (k + 1) // CHUNKS):
            skew(c + 1)
            shifted[c] = shifts(c)
        skew(2 + (owned - 2) * (k + 1) // CHUNKS)
        for h in range(0, channels, block):
            traces = held[:, h : h + block, k * width : (k + 1) * width].reshape(cols, width)
            lines = jnp.dot(mix[...], traces, preferred_element_type=F32).astype(BF16)
            for c in range(owned):
                mixed[c, h : h + block, k * width : (k + 1) * width] = lines[c * block : (c + 1) * block]
    for c in range(owned):
        kernel = shifted[c] if c < early else shifts(c)
        out[c] = jnp.dot(mixed[c], kernel, preferred_element_type=F32).astype(out.dtype)


def decode(inputs, shape, owned, codes, lags, step, dtype, first):
    sweeps, channels, samples = shape
    block = min(channels, 256 // sweeps)
    early = min(4, owned)
    out_shape = [pltpu.VMEM((owned, channels, lags), dtype)]
    scratch = [
        pltpu.VMEM((owned * block, sweeps * block), BF16),
        pltpu.VMEM((owned, SKEW, samples + lags), BF16),
        pltpu.VMEM((owned, channels, samples), BF16),
        pltpu.VMEM((early, samples, lags), BF16),
    ]
    if first:
        vib, hadamard, pilots, owner, live, _ = inputs
        inputs = [pltpu.with_memory_space_constraint(x, pltpu.HBM) for x in inputs]
        out_shape += [
            pltpu.VMEM(shape, BF16),
            pltpu.VMEM(hadamard.shape, jnp.int32),
            pltpu.VMEM((codes, samples + lags), F32),
            pltpu.VMEM((owned, channels, lags), F32),
        ]
        scratch += [
            pltpu.SemaphoreType.DMA((CHUNKS + 5,)),
            pltpu.SMEM(vib.shape, jnp.int32),
            pltpu.VMEM(pilots.shape, BF16),
            pltpu.VMEM(owner.shape, jnp.int32),
            pltpu.VMEM(live.shape, jnp.int32),
            pltpu.VMEM((pilots.shape[0], samples + lags), F32),
        ]
    return pl.pallas_call(
        functools.partial(decode_kernel, step=step, first=first),
        out_shape=out_shape,
        in_specs=[HBM if first else VMEM] * len(inputs),
        out_specs=[VMEM] * len(out_shape),
        scratch_shapes=scratch,
        compiler_params=pltpu.CompilerParams(vmem_limit_bytes=VMEM_LIMIT),
        cost_estimate=pl.CostEstimate(flops=8 * 10**9, bytes_accessed=math.prod(shape) * 2, transcendentals=0),
        name=f"decode_{step}",
    )(*inputs)


def tail_kernel(weight, own, *refs, parts, norm, factor, radix):
    others, (filters, targets, responses, keep, *sends, terms) = refs[:parts], refs[parts:]
    owned = own.shape[0]
    shares, _, share_rows, _ = terms.shape
    every = range(owned)
    partial = [own[c] for c in every]
    for other in others:
        partial = [partial[c] + other[c].astype(F32) for c in every]
    decoded = [(norm * p).astype(BF16) for p in partial]
    response = [jnp.dot(decoded[c], filters[c], preferred_element_type=F32) for c in every]
    for c in every:
        responses[c] = response[c]
    residual = [(weight[c] * (response[c] - targets[c].astype(F32))).astype(BF16) for c in every]
    grad = [
        factor * lax.dot_general(decoded[c], residual[c], (((0,), (0,)), ((), ())), preferred_element_type=F32)
        for c in every
    ]
    for c in every:
        for d in range(shares):
            terms[d, c] = grad[c][d * share_rows : (d + 1) * share_rows]
    digit = lax.rem(lax.axis_index("recv"), radix)
    for i in range(shares // radix):
        keep[i] = terms[i * radix + digit]
        for k, send in enumerate(sends):
            send[i] = terms[i * radix + (digit ^ (k + 1))].astype(BF16)


def rounds(size):
    parts = [2]
    while math.prod(parts) < size:
        parts.append(4 if size // math.prod(parts) % 4 == 0 else 2)
    return parts


def local(records, pilots, hadamard, code_vibrator, owner_map, live_mask, filters, targets):
    groups = lax.axis_size("sweep")
    size = lax.axis_size("recv")
    codes = hadamard.shape[1]
    owned, lags, _ = filters.shape
    channels = records.shape[1]
    received = []
    inputs = (code_vibrator, hadamard, pilots, owner_map.reshape(1, channels), live_mask.reshape(1, channels), records)
    first = True
    for step in list(range(1, groups)) + [0]:
        dtype = BF16 if step else F32
        part, *extra = decode(inputs, records.shape, owned, codes, lags, step, dtype, first)
        if first:
            *inputs, weight = extra
            first = False
        if step:
            received.append(lax.ppermute(part, "sweep", [(i, (i + step) % groups) for i in range(groups)]))
    share_rows = lags // size
    radices = rounds(size)
    piece = (size // radices[0], owned, share_rows, lags)
    responses, held, *sent = pl.pallas_call(
        functools.partial(
            tail_kernel,
            parts=len(received),
            norm=1.0 / math.sqrt(codes),
            factor=1.0 / math.sqrt(channels * size),
            radix=radices[0],
        ),
        out_shape=[pltpu.VMEM((owned, channels, lags), F32), pltpu.VMEM(piece, F32)]
        + [pltpu.VMEM(piece, BF16)] * (radices[0] - 1),
        in_specs=[VMEM] * (4 + len(received)),
        out_specs=[VMEM] * (1 + radices[0]),
        scratch_shapes=[pltpu.VMEM((size, owned, share_rows, lags), F32)],
        compiler_params=pltpu.CompilerParams(vmem_limit_bytes=8 * 2**20),
        name="tail",
    )(weight, part, *received, filters, targets)
    me = lax.axis_index("recv")
    stride = 1
    for j, radix in enumerate(radices):
        for k, value in enumerate(sent):
            pairs = [(i, i ^ (k + 1) * stride) for i in range(size)]
            held = held + lax.ppermute(value, "recv", pairs).astype(F32)
        stride *= radix
        if j + 1 < len(radices):
            digit = (me // stride) & (radices[j + 1] - 1)
            grid = held.reshape((-1, radices[j + 1]) + held.shape[1:])
            sent = [
                lax.dynamic_index_in_dim(grid, digit ^ k, 1, keepdims=False).astype(BF16)
                for k in range(1, radices[j + 1])
            ]
            held = lax.dynamic_index_in_dim(grid, digit, 1, keepdims=False)
    return (responses, held[0])


def solution(mesh):
    in_specs = (
        P("sweep", "recv", None),
        P(),
        P(),
        P(),
        P("recv"),
        P("recv"),
        P("sweep", None, None),
        P("sweep", "recv", None),
    )
    out_specs = (P("sweep", "recv", None), P("sweep", "recv", None))
    return jax.shard_map(local, mesh=mesh, in_specs=in_specs, out_specs=out_specs, check_vma=False)
```

```python
import functools
import math

import jax
import jax.numpy as jnp
from jax import lax
from jax.experimental import pallas as pl
from jax.experimental.pallas import tpu as pltpu
from jax.sharding import PartitionSpec as P

BF16 = jnp.bfloat16
F32 = jnp.float32
SMEM = pl.BlockSpec(memory_space=pltpu.SMEM)
VMEM = pl.BlockSpec(memory_space=pltpu.VMEM)
HBM = pl.BlockSpec(memory_space=pltpu.HBM)
SKEW = 16
CUTS = (1, 1, 2)
VMEM_LIMIT = 28 * 2**20


def iota(shape, axis):
    return lax.broadcasted_iota(jnp.int32, shape, axis)


def column(row):
    size = row.shape[1]
    eye = iota((size, size), 0) == iota((size, size), 1)
    return jnp.sum(jnp.where(eye, jnp.broadcast_to(row.astype(F32), (size, size)), 0.0), axis=1, keepdims=True)


def decode_kernel(*refs, step, first):
    if first:
        (vib, hadamard, pilots, records), (out, held, signs_v, backward) = refs[:4], refs[4:8]
        mix, skewed, mixed, shifted, sems, vib_s, pilots_v = refs[8:]
    else:
        (vib, owner, live, held, signs_v, backward), (out, weight) = refs[:6], refs[6:8]
        mix, skewed, mixed, shifted, sems, vib_s = refs[8:]
    sweeps, channels, samples = held.shape
    owned, _, lags = out.shape
    all_sweeps, codes = signs_v.shape
    block = mix.shape[1] // sweeps
    shift = block.bit_length() - 1
    early = shifted.shape[0]
    bounds = [samples * sum(CUTS[:k]) // sum(CUTS) for k in range(len(CUTS) + 1)]
    mine = lax.axis_index("sweep")
    first_sweep = mine * sweeps
    first_code = lax.rem(mine + step, lax.axis_size("sweep")) * owned

    def fetch(k):
        cols = pl.ds(bounds[k], bounds[k + 1] - bounds[k])
        return pltpu.make_async_copy(records.at[:, :, cols], held.at[:, :, cols], sems.at[k])

    if first:
        small = [(hadamard, signs_v), (pilots, pilots_v), (vib, vib_s)]
        small = [pltpu.make_async_copy(x, y, sems.at[len(CUTS) + i]) for i, (x, y) in enumerate(small)]
        for copy in small:
            copy.start()
        for k in range(len(CUTS)):
            fetch(k).start()
        for copy in small:
            copy.wait()

    else:
        copy = pltpu.make_async_copy(vib, vib_s, sems.at[0])
        copy.start()

    signs = signs_v[...].astype(F32).astype(BF16)
    rows, cols = mix.shape
    pick_code = (iota((rows, codes), 1) == first_code + (iota((rows, codes), 0) >> shift)).astype(F32).astype(BF16)
    pick_sweep = (iota((all_sweeps, cols), 0) == first_sweep + (iota((all_sweeps, cols), 1) >> shift)).astype(F32).astype(BF16)
    by_code = lax.dot_general(pick_code, signs, (((1,), (1,)), ((), ())), preferred_element_type=F32).astype(BF16)
    spread = jnp.dot(by_code, pick_sweep, preferred_element_type=F32)
    same = (iota((rows, cols), 0) & (block - 1)) == (iota((rows, cols), 1) & (block - 1))
    mix[...] = jnp.where(same, spread, 0.0).astype(BF16)

    if first:
        vibrators, length = pilots.shape
        flip = (iota((lags, lags), 0) + iota((lags, lags), 1) == lags - 1).astype(F32).astype(BF16)
        pieces = jnp.concatenate([pilots_v[:, j : j + lags] for j in range(0, length, lags)], axis=0)
        pieces = jnp.dot(pieces, flip, preferred_element_type=F32)
        for j in range(samples // lags + 1):
            source = (samples // lags - 1 - j) * vibrators
            inside = 0 <= source < pieces.shape[0]
            backward[:, j * lags : (j + 1) * lags] = (
                pieces[source : source + vibrators] if inside else jnp.zeros((vibrators, lags), F32)
            )
    else:
        copy.wait()
    made = 0

    def skew(upto):
        nonlocal made
        while made < min(upto, owned):
            row = backward[pl.ds(vib_s[first_code + made], 1), :]
            wide = jnp.broadcast_to(row, (SKEW, samples + lags))
            skewed[made] = pltpu.roll(wide, 1, 1, stride=1, stride_axis=0).astype(BF16)
            made += 1

    def shifts(c):
        phases = [skewed[c, :, lags - j : lags - j + samples] for j in range(0, lags, SKEW)]
        return jnp.concatenate(
            [p[:, samples - u - lags : samples - u] for u in range(0, samples, lags) for p in phases], axis=0
        )

    skew(2)
    cuts = bounds if first else [0, samples // 2, samples]
    for k in range(len(cuts) - 1):
        start, stop = cuts[k], cuts[k + 1]
        if first:
            fetch(k).wait()
        for c in range(early * start // samples, early * stop // samples):
            skew(c + 1)
            shifted[c] = shifts(c)
        skew(2 + (owned - 2) * stop // samples)
        for h in range(0, channels, block):
            traces = held[:, h : h + block, start:stop].reshape(cols, stop - start)
            lines = jnp.dot(mix[...], traces, preferred_element_type=F32).astype(BF16)
            for c in range(owned):
                mixed[c, h : h + block, start:stop] = lines[c * block : (c + 1) * block]
    for c in range(owned):
        kernel = shifted[c] if c < early else shifts(c)
        out[c] = jnp.dot(mixed[c], kernel, preferred_element_type=F32).astype(out.dtype)
    if not first:
        owner_c, live_c = column(owner[...]), column(live[...])
        for c in range(owned):
            match = (owner_c == vib_s[first_code + c].astype(F32)).astype(F32)
            weight[c] = jnp.broadcast_to(live_c * (0.25 + match), weight.shape[1:])


def decode(inputs, shape, owned, codes, lags, step, dtype, first):
    sweeps, channels, samples = shape
    block = min(channels, 256 // sweeps)
    early = min(4, owned)
    out_shape = [pltpu.VMEM((owned, channels, lags), dtype)]
    scratch = [
        pltpu.VMEM((owned * block, sweeps * block), BF16),
        pltpu.VMEM((owned, SKEW, samples + lags), BF16),
        pltpu.VMEM((owned, channels, samples), BF16),
        pltpu.VMEM((early, samples, lags), BF16),
    ]
    vib = inputs[0]
    if first:
        _, hadamard, pilots, _ = inputs
        inputs = [pltpu.with_memory_space_constraint(x, pltpu.HBM) for x in inputs]
        specs = [HBM] * 4
        out_shape += [
            pltpu.VMEM(shape, BF16),
            pltpu.VMEM(hadamard.shape, jnp.int32),
            pltpu.VMEM((pilots.shape[0], samples + lags), F32),
        ]
        scratch += [
            pltpu.SemaphoreType.DMA((len(CUTS) + 3,)),
            pltpu.SMEM(vib.shape, jnp.int32),
            pltpu.VMEM(pilots.shape, BF16),
        ]
    else:
        inputs = [pltpu.with_memory_space_constraint(vib, pltpu.HBM), *inputs[1:]]
        specs = [HBM] + [VMEM] * (len(inputs) - 1)
        out_shape += [pltpu.VMEM((owned, channels, lags), F32)]
        scratch += [pltpu.SemaphoreType.DMA((1,)), pltpu.SMEM(vib.shape, jnp.int32)]
    return pl.pallas_call(
        functools.partial(decode_kernel, step=step, first=first),
        out_shape=out_shape,
        in_specs=specs,
        out_specs=[VMEM] * len(out_shape),
        scratch_shapes=scratch,
        compiler_params=pltpu.CompilerParams(vmem_limit_bytes=VMEM_LIMIT),
        cost_estimate=pl.CostEstimate(flops=8 * 10**9, bytes_accessed=math.prod(shape) * 2, transcendentals=0),
        name=f"decode_{step}",
    )(*inputs)


def tail_kernel(weight, own, *refs, parts, norm, factor, radix):
    others, (filters, targets, responses, keep, *sends, terms) = refs[:parts], refs[parts:]
    owned = own.shape[0]
    shares, _, share_rows, _ = terms.shape
    every = range(owned)
    partial = [own[c] for c in every]
    for other in others:
        partial = [partial[c] + other[c].astype(F32) for c in every]
    decoded = [(norm * p).astype(BF16) for p in partial]
    response = [jnp.dot(decoded[c], filters[c], preferred_element_type=F32) for c in every]
    for c in every:
        responses[c] = response[c]
    residual = [(weight[c] * (response[c] - targets[c].astype(F32))).astype(BF16) for c in every]
    grad = [
        factor * lax.dot_general(decoded[c], residual[c], (((0,), (0,)), ((), ())), preferred_element_type=F32)
        for c in every
    ]
    for c in every:
        for d in range(shares):
            terms[d, c] = grad[c][d * share_rows : (d + 1) * share_rows]
    digit = lax.rem(lax.axis_index("recv"), radix)
    for i in range(shares // radix):
        keep[i] = terms[i * radix + digit]
        for k, send in enumerate(sends):
            send[i] = terms[i * radix + (digit ^ (k + 1))].astype(BF16)


def rounds(size):
    parts = [2]
    while math.prod(parts) < size:
        parts.append(4 if size // math.prod(parts) % 4 == 0 else 2)
    return parts


def local(records, pilots, hadamard, code_vibrator, owner_map, live_mask, filters, targets):
    groups = lax.axis_size("sweep")
    size = lax.axis_size("recv")
    codes = hadamard.shape[1]
    owned, lags, _ = filters.shape
    channels = records.shape[1]
    received = []
    inputs = (code_vibrator, hadamard, pilots, records)
    first = True
    for step in list(range(1, groups)) + [0]:
        dtype = BF16 if step else F32
        part, *extra = decode(inputs, records.shape, owned, codes, lags, step, dtype, first)
        if first:
            row = (1, channels)
            inputs = (code_vibrator, owner_map.reshape(row), live_mask.reshape(row), *extra)
            first = False
        if step:
            received.append(lax.ppermute(part, "sweep", [(i, (i + step) % groups) for i in range(groups)]))
    weight = extra[0]
    share_rows = lags // size
    radices = rounds(size)
    piece = (size // radices[0], owned, share_rows, lags)
    responses, held, *sent = pl.pallas_call(
        functools.partial(
            tail_kernel,
            parts=len(received),
            norm=1.0 / math.sqrt(codes),
            factor=1.0 / math.sqrt(channels * size),
            radix=radices[0],
        ),
        out_shape=[pltpu.VMEM((owned, channels, lags), F32), pltpu.VMEM(piece, F32)]
        + [pltpu.VMEM(piece, BF16)] * (radices[0] - 1),
        in_specs=[VMEM] * (4 + len(received)),
        out_specs=[VMEM] * (1 + radices[0]),
        scratch_shapes=[pltpu.VMEM((size, owned, share_rows, lags), F32)],
        compiler_params=pltpu.CompilerParams(vmem_limit_bytes=8 * 2**20),
        name="tail",
    )(weight, part, *received, filters, targets)
    me = lax.axis_index("recv")
    stride = 1
    for j, radix in enumerate(radices):
        for k, value in enumerate(sent):
            pairs = [(i, i ^ (k + 1) * stride) for i in range(size)]
            held = held + lax.ppermute(value, "recv", pairs).astype(F32)
        stride *= radix
        if j + 1 < len(radices):
            digit = (me // stride) & (radices[j + 1] - 1)
            grid = held.reshape((-1, radices[j + 1]) + held.shape[1:])
            sent = [
                lax.dynamic_index_in_dim(grid, digit ^ k, 1, keepdims=False).astype(BF16)
                for k in range(1, radices[j + 1])
            ]
            held = lax.dynamic_index_in_dim(grid, digit, 1, keepdims=False)
    return (responses, held[0])


def solution(mesh):
    in_specs = (
        P("sweep", "recv", None),
        P(),
        P(),
        P(),
        P("recv"),
        P("recv"),
        P("sweep", None, None),
        P("sweep", "recv", None),
    )
    out_specs = (P("sweep", "recv", None), P("sweep", "recv", None))
    return jax.shard_map(local, mesh=mesh, in_specs=in_specs, out_specs=out_specs, check_vma=False)
```

```python
import functools
import math

import jax
import jax.numpy as jnp
from jax import lax
from jax.experimental import pallas as pl
from jax.experimental.pallas import tpu as pltpu
from jax.sharding import PartitionSpec as P

BF16 = jnp.bfloat16
F32 = jnp.float32
SMEM = pl.BlockSpec(memory_space=pltpu.SMEM)
VMEM = pl.BlockSpec(memory_space=pltpu.VMEM)
HBM = pl.BlockSpec(memory_space=pltpu.HBM)
SKEW = 16
CUTS = (1, 1, 2)
VMEM_LIMIT = 28 * 2**20


def iota(shape, axis):
    return lax.broadcasted_iota(jnp.int32, shape, axis)


def column(row):
    size = row.shape[1]
    eye = iota((size, size), 0) == iota((size, size), 1)
    return jnp.sum(jnp.where(eye, jnp.broadcast_to(row.astype(F32), (size, size)), 0.0), axis=1, keepdims=True)


def decode_kernel(*refs, step, first):
    if first:
        (vib, hadamard, pilots, records), (out, held, signs_v, backward) = refs[:4], refs[4:8]
        mix, skewed, mixed, shifted, sems, vib_s, pilots_v = refs[8:]
    else:
        (vib, owner, live, held, signs_v, backward), (out, weight) = refs[:6], refs[6:8]
        mix, skewed, mixed, shifted, sems, vib_s = refs[8:]
    sweeps, channels, samples = held.shape
    owned, _, lags = out.shape
    all_sweeps, codes = signs_v.shape
    block = mix.shape[1] // sweeps
    shift = block.bit_length() - 1
    early = shifted.shape[0]
    bounds = [samples * sum(CUTS[:k]) // sum(CUTS) for k in range(len(CUTS) + 1)]
    mine = lax.axis_index("sweep")
    first_sweep = mine * sweeps
    first_code = lax.rem(mine + step, lax.axis_size("sweep")) * owned

    def fetch(k):
        cols = pl.ds(bounds[k], bounds[k + 1] - bounds[k])
        return pltpu.make_async_copy(records.at[:, :, cols], held.at[:, :, cols], sems.at[k])

    if first:
        small = [(hadamard, signs_v), (pilots, pilots_v), (vib, vib_s)]
        small = [pltpu.make_async_copy(x, y, sems.at[len(CUTS) + i]) for i, (x, y) in enumerate(small)]
        for copy in small:
            copy.start()
        for k in range(len(CUTS)):
            fetch(k).start()
        for copy in small:
            copy.wait()

    else:
        copy = pltpu.make_async_copy(vib, vib_s, sems.at[0])
        copy.start()

    signs = signs_v[...].astype(F32).astype(BF16)
    rows, cols = mix.shape
    pick_code = (iota((rows, codes), 1) == first_code + (iota((rows, codes), 0) >> shift)).astype(F32).astype(BF16)
    pick_sweep = (iota((all_sweeps, cols), 0) == first_sweep + (iota((all_sweeps, cols), 1) >> shift)).astype(F32).astype(BF16)
    by_code = lax.dot_general(pick_code, signs, (((1,), (1,)), ((), ())), preferred_element_type=F32).astype(BF16)
    spread = jnp.dot(by_code, pick_sweep, preferred_element_type=F32)
    same = (iota((rows, cols), 0) & (block - 1)) == (iota((rows, cols), 1) & (block - 1))
    mix[...] = jnp.where(same, spread, 0.0).astype(BF16)

    if first:
        vibrators, length = pilots.shape
        flip = (iota((lags, lags), 0) + iota((lags, lags), 1) == lags - 1).astype(F32).astype(BF16)
        pieces = jnp.concatenate([pilots_v[:, j : j + lags] for j in range(0, length, lags)], axis=0)
        pieces = jnp.dot(pieces, flip, preferred_element_type=F32)
        for j in range(samples // lags + 1):
            source = (samples // lags - 1 - j) * vibrators
            inside = 0 <= source < pieces.shape[0]
            backward[:, j * lags : (j + 1) * lags] = (
                pieces[source : source + vibrators] if inside else jnp.zeros((vibrators, lags), F32)
            )
    else:
        copy.wait()
    made = 0

    def skew(upto):
        nonlocal made
        while made < min(upto, owned):
            row = backward[pl.ds(vib_s[first_code + made], 1), :]
            wide = jnp.broadcast_to(row, (SKEW, samples + lags))
            skewed[made] = pltpu.roll(wide, 1, 1, stride=1, stride_axis=0).astype(BF16)
            made += 1

    def shifts(c):
        phases = [skewed[c, :, lags - j : lags - j + samples] for j in range(0, lags, SKEW)]
        return jnp.concatenate(
            [p[:, samples - u - lags : samples - u] for u in range(0, samples, lags) for p in phases], axis=0
        )

    skew(2)
    cuts = bounds if first else [0, samples // 2, samples]
    for k in range(len(cuts) - 1):
        start, stop = cuts[k], cuts[k + 1]
        if first:
            fetch(k).wait()
        for c in range(early * start // samples, early * stop // samples):
            skew(c + 1)
            shifted[c] = shifts(c)
        skew(2 + (owned - 2) * stop // samples)
        for h in range(0, channels, block):
            traces = held[:, h : h + block, start:stop].reshape(cols, stop - start)
            lines = jnp.dot(mix[...], traces, preferred_element_type=F32).astype(BF16)
            for c in range(owned):
                mixed[c, h : h + block, start:stop] = lines[c * block : (c + 1) * block]
    for c in range(owned):
        kernel = shifted[c] if c < early else shifts(c)
        out[c] = jnp.dot(mixed[c], kernel, preferred_element_type=F32).astype(out.dtype)
    if not first:
        owner_c, live_c = column(owner[...]), column(live[...])
        for c in range(owned):
            match = (owner_c == vib_s[first_code + c].astype(F32)).astype(F32)
            weight[c] = jnp.broadcast_to(live_c * (0.25 + match), weight.shape[1:])


def decode(inputs, shape, owned, codes, lags, step, dtype, first):
    sweeps, channels, samples = shape
    block = min(channels, 256 // sweeps)
    early = min(4, owned)
    out_shape = [pltpu.VMEM((owned, channels, lags), dtype)]
    scratch = [
        pltpu.VMEM((owned * block, sweeps * block), BF16),
        pltpu.VMEM((owned, SKEW, samples + lags), BF16),
        pltpu.VMEM((owned, channels, samples), BF16),
        pltpu.VMEM((early, samples, lags), BF16),
    ]
    vib = inputs[0]
    if first:
        _, hadamard, pilots, _ = inputs
        inputs = [pltpu.with_memory_space_constraint(x, pltpu.HBM) for x in inputs]
        specs = [HBM] * 4
        out_shape += [
            pltpu.VMEM(shape, BF16),
            pltpu.VMEM(hadamard.shape, jnp.int32),
            pltpu.VMEM((pilots.shape[0], samples + lags), F32),
        ]
        scratch += [
            pltpu.SemaphoreType.DMA((len(CUTS) + 3,)),
            pltpu.SMEM(vib.shape, jnp.int32),
            pltpu.VMEM(pilots.shape, BF16),
        ]
    else:
        inputs = [pltpu.with_memory_space_constraint(vib, pltpu.HBM), *inputs[1:]]
        specs = [HBM] + [VMEM] * (len(inputs) - 1)
        out_shape += [pltpu.VMEM((owned, channels, lags), F32)]
        scratch += [pltpu.SemaphoreType.DMA((1,)), pltpu.SMEM(vib.shape, jnp.int32)]
    return pl.pallas_call(
        functools.partial(decode_kernel, step=step, first=first),
        out_shape=out_shape,
        in_specs=specs,
        out_specs=[VMEM] * len(out_shape),
        scratch_shapes=scratch,
        compiler_params=pltpu.CompilerParams(vmem_limit_bytes=VMEM_LIMIT),
        cost_estimate=pl.CostEstimate(flops=8 * 10**9, bytes_accessed=math.prod(shape) * 2, transcendentals=0),
        name=f"decode_{step}",
    )(*inputs)


def tail_kernel(weight, own, *refs, parts, norm, factor, radix):
    others, (filters, targets, responses, keep, *sends) = refs[:parts], refs[parts:]
    owned = own.shape[0]
    shares, share_rows = keep.shape[0] * radix, keep.shape[2]
    every = range(owned)
    partial = [own[c] for c in every]
    for other in others:
        partial = [partial[c] + other[c].astype(F32) for c in every]
    decoded = [(norm * p).astype(BF16) for p in partial]
    response = [jnp.dot(decoded[c], filters[c], preferred_element_type=F32) for c in every]
    for c in every:
        responses[c] = response[c]
    residual = [(weight[c] * (response[c] - targets[c].astype(F32))).astype(BF16) for c in every]
    grad = [
        factor * lax.dot_general(decoded[c], residual[c], (((0,), (0,)), ((), ())), preferred_element_type=F32)
        for c in every
    ]
    odd = lax.rem(lax.axis_index("recv"), radix) == 1
    for c in every:
        for i in range(shares // radix):
            low, high = (grad[c][d * share_rows : (d + 1) * share_rows] for d in (2 * i, 2 * i + 1))
            keep[i, c] = jnp.where(odd, high, low)
            sends[0][i, c] = jnp.where(odd, low, high).astype(BF16)


def rounds(size):
    parts = [2]
    while math.prod(parts) < size:
        parts.append(4 if size // math.prod(parts) % 4 == 0 else 2)
    return parts


def local(records, pilots, hadamard, code_vibrator, owner_map, live_mask, filters, targets):
    groups = lax.axis_size("sweep")
    size = lax.axis_size("recv")
    codes = hadamard.shape[1]
    owned, lags, _ = filters.shape
    channels = records.shape[1]
    received = []
    inputs = (code_vibrator, hadamard, pilots, records)
    first = True
    for step in list(range(1, groups)) + [0]:
        dtype = BF16 if step else F32
        part, *extra = decode(inputs, records.shape, owned, codes, lags, step, dtype, first)
        if first:
            row = (1, channels)
            inputs = (code_vibrator, owner_map.reshape(row), live_mask.reshape(row), *extra)
            first = False
        if step:
            received.append(lax.ppermute(part, "sweep", [(i, (i + step) % groups) for i in range(groups)]))
    weight = extra[0]
    share_rows = lags // size
    radices = rounds(size)
    piece = (size // radices[0], owned, share_rows, lags)
    responses, held, *sent = pl.pallas_call(
        functools.partial(
            tail_kernel,
            parts=len(received),
            norm=1.0 / math.sqrt(codes),
            factor=1.0 / math.sqrt(channels * size),
            radix=radices[0],
        ),
        out_shape=[pltpu.VMEM((owned, channels, lags), F32), pltpu.VMEM(piece, F32)]
        + [pltpu.VMEM(piece, BF16)] * (radices[0] - 1),
        in_specs=[VMEM] * (4 + len(received)),
        out_specs=[VMEM] * (1 + radices[0]),
        compiler_params=pltpu.CompilerParams(vmem_limit_bytes=8 * 2**20),
        name="tail",
    )(weight, part, *received, filters, targets)
    me = lax.axis_index("recv")
    stride = 1
    for j, radix in enumerate(radices):
        for k, value in enumerate(sent):
            pairs = [(i, i ^ (k + 1) * stride) for i in range(size)]
            held = held + lax.ppermute(value, "recv", pairs).astype(F32)
        stride *= radix
        if j + 1 < len(radices):
            digit = (me // stride) & (radices[j + 1] - 1)
            grid = held.reshape((-1, radices[j + 1]) + held.shape[1:])
            sent = [
                lax.dynamic_index_in_dim(grid, digit ^ k, 1, keepdims=False).astype(BF16)
                for k in range(1, radices[j + 1])
            ]
            held = lax.dynamic_index_in_dim(grid, digit, 1, keepdims=False)
    return (responses, held[0])


def solution(mesh):
    in_specs = (
        P("sweep", "recv", None),
        P(),
        P(),
        P(),
        P("recv"),
        P("recv"),
        P("sweep", None, None),
        P("sweep", "recv", None),
    )
    out_specs = (P("sweep", "recv", None), P("sweep", "recv", None))
    return jax.shard_map(local, mesh=mesh, in_specs=in_specs, out_specs=out_specs, check_vma=False)
```
